32 devices in a mesh: dp: 8 (over z, x), seq: 4 (over y, core).
Axes of the slice: x: 2, y: 2, z: 4, core: 2. Of those that a mesh axis runs over, the one named last changes fastest.
Arguments:
- embeds: bfloat16 [16, 736, 1152], P('dp', 'seq'), may hold values from -6 to 6
- image_counts: int32 [8], P('dp'), may hold values from 1 to 2, as said below
- norm1_gain: float32 [1152], P('seq'), may hold values from 0.5 to 1.5
- norm1_bias: float32 [1152], P('seq'), may hold values from -3 to 3
- query_weight: float32 [1152, 1152], P('dp', 'seq'), may hold values from -0.1875 to 0.1875
- query_bias: float32 [1152], P('seq'), may hold values from -3 to 3
- key_weight: float32 [1152, 1152], P('dp', 'seq'), may hold values from -0.1875 to 0.1875
- value_weight: float32 [1152, 1152], P('dp', 'seq'), may hold values from -0.1875 to 0.1875
- value_bias: float32 [1152], P('seq'), may hold values from -3 to 3
- out_weight: float32 [1152, 1152], P('dp', 'seq'), may hold values from -1.5 to 1.5
- out_bias: float32 [1152], P('seq'), may hold values from -3 to 3
- norm2_gain: float32 [1152], P('seq'), may hold values from 0.5 to 1.5
- norm2_bias: float32 [1152], P('seq'), may hold values from -3 to 3
- fc1_weight: float32 [1152, 4304], P('dp', 'seq'), may hold values from -0.1875 to 0.1875
- fc1_bias: float32 [4304], P('seq'), may hold values from -3 to 3
- fc2_weight: float32 [1152, 4304], P('dp', 'seq'), may hold values from -0.09375 to 0.09375
- fc2_bias: float32 [1152], P('seq'), may hold values from -3 to 3
- out_grad: bfloat16 [16, 736, 1152], P('dp', 'seq'), may hold values from -6 to 6
Outputs:
- output: bfloat16 [16, 736, 1152], P('dp', 'seq')
- embeds_grad: bfloat16 [16, 736, 1152], P('dp', 'seq')
- norm1_gain_grad: float32 [1152], P('seq')
- norm1_bias_grad: float32 [1152], P('seq')
- query_weight_grad: float32 [1152, 1152], P('dp', 'seq')
- query_bias_grad: float32 [1152], P('seq')
- key_weight_grad: float32 [1152, 1152], P('dp', 'seq')
- value_weight_grad: float32 [1152, 1152], P('dp', 'seq')
- value_bias_grad: float32 [1152], P('seq')
- out_weight_grad: float32 [1152, 1152], P('dp', 'seq')
- out_bias_grad: float32 [1152], P('seq')
- norm2_gain_grad: float32 [1152], P('seq')
- norm2_bias_grad: float32 [1152], P('seq')
- fc1_weight_grad: float32 [1152, 4304], P('dp', 'seq')
- fc1_bias_grad: float32 [4304], P('seq')
- fc2_weight_grad: float32 [1152, 4304], P('dp', 'seq')
- fc2_bias_grad: float32 [1152], P('seq')
The draws below stay inside these ranges and needn't reach their ends.
Inputs may be any that keep to these rules, and one draw needn't show every extreme that they name: The first image_counts[g] of group g's 2 image slots hold images, the others are empty; some group holds 2.
All inputs are finite; a program needn't handle non-finite values.
Results may differ from the reference program's by a relative error of at most 0.017.
Values may be sent and summed in bfloat16 or wider, within the bound.
A program may use at most 192 MiB of HBM per device.

```python
import jax
import jax.numpy as jnp
from jax import lax

D = 1152
HEADS = 16
HEAD_DIM = 72
FF = 4304
SLOTS = 736
VALID = 729
IMG_DEV = 2
DP_GROUPS = 8
IMAGES = 16


def draw_image_counts(key, part):
    base_key, pick_key = jax.random.split(jax.random.fold_in(key, 17))
    drawn = jax.random.randint(base_key, (DP_GROUPS,), 1, IMG_DEV + 1)
    chosen = jax.random.randint(pick_key, (), 0, DP_GROUPS)
    return jnp.where(jnp.arange(DP_GROUPS) == chosen, IMG_DEV, drawn).astype(jnp.int32)


def level_of(rng, dims, shards, least, largest):
    def one(position, shards_of):
        steps = jax.random.uniform(jax.random.fold_in(jax.random.fold_in(rng, 6), position), (shards_of,), jnp.float32, least / len(shards), largest / len(shards))
        return jnp.repeat(jnp.exp(steps), dims[position] // shards_of).reshape((-1,) + (1,) * (len(dims) - position - 1))

    level = one(*shards[0])
    for cut in shards[1:]:
        level = level * one(*cut)
    return level


def normal_values(rng, shape, scale, limit, shards=(), held_as=jnp.bfloat16):
    values = scale * jax.random.normal(rng, shape, jnp.float32)
    if shards:
        values = values * level_of(rng, shape, shards, -0.22, 0.18)
    return jnp.clip(values, -limit, limit).astype(held_as)


def setup_inputs(seed: int = 0) -> dict:
    splits = jax.random.split(jax.random.key(seed), 19)
    embeds = normal_values(splits[0], (IMAGES, SLOTS, D), 1.0, 6.0, ((0, 8), (1, 4)))
    image_counts = draw_image_counts(jax.random.fold_in(splits[18], 71), 0)
    norm1_gain = jnp.clip(1.0 + 0.1 * jax.random.normal(splits[2], (D,), jnp.float32), 0.5, 1.5)
    norm1_bias = normal_values(splits[3], (D,), 0.5, 3.0, ((0, 4),), jnp.float32)
    query_weight = normal_values(splits[4], (D, D), D ** -0.5, 0.1875, ((0, 8), (1, 4)), jnp.float32)
    query_bias = normal_values(splits[5], (D,), 0.5, 3.0, ((0, 4),), jnp.float32)
    key_weight = normal_values(splits[6], (D, D), D ** -0.5, 0.1875, ((0, 8), (1, 4)), jnp.float32)
    value_weight = normal_values(splits[7], (D, D), D ** -0.5, 0.1875, ((0, 8), (1, 4)), jnp.float32)
    value_bias = normal_values(splits[8], (D,), 0.5, 3.0, ((0, 4),), jnp.float32)
    out_weight = normal_values(splits[9], (D, D), (D // 64) ** -0.5, 1.5, ((0, 8), (1, 4)), jnp.float32)
    out_bias = normal_values(splits[10], (D,), 0.5, 3.0, ((0, 4),), jnp.float32)
    norm2_gain = jnp.clip(1.0 + 0.1 * jax.random.normal(splits[11], (D,), jnp.float32), 0.5, 1.5)
    norm2_bias = normal_values(splits[12], (D,), 0.5, 3.0, ((0, 4),), jnp.float32)
    fc1_weight = normal_values(splits[13], (D, FF), D ** -0.5, 0.1875, ((0, 8), (1, 4)), jnp.float32)
    fc1_bias = normal_values(splits[14], (FF,), 0.5, 3.0, ((0, 4),), jnp.float32)
    fc2_weight = normal_values(splits[15], (D, FF), FF ** -0.5, 0.09375, ((0, 8), (1, 4)), jnp.float32)
    fc2_bias = normal_values(splits[16], (D,), 0.5, 3.0, ((0, 4),), jnp.float32)
    out_grad = normal_values(splits[17], (IMAGES, SLOTS, D), 1.0, 6.0, ((0, 8), (1, 4)))
    return {"embeds": embeds, "image_counts": image_counts, "norm1_gain": norm1_gain, "norm1_bias": norm1_bias, "query_weight": query_weight, "query_bias": query_bias, "key_weight": key_weight, "value_weight": value_weight, "value_bias": value_bias, "out_weight": out_weight, "out_bias": out_bias, "norm2_gain": norm2_gain, "norm2_bias": norm2_bias, "fc1_weight": fc1_weight, "fc1_bias": fc1_bias, "fc2_weight": fc2_weight, "fc2_bias": fc2_bias, "out_grad": out_grad}


EPSILON = 1e-06
NEGATIVE = -1000000000.0
HIGHEST_MODE = lax.Precision.HIGHEST

@jax.custom_vjp
def low(v):
    return lax.optimization_barrier(v.astype(jnp.bfloat16)).astype(jnp.float32)

@jax.custom_vjp
def low_back(v):
    return v

def low_keep(v):
    return (low(v), None)

def low_pass(kept, grad):
    return (grad,)

def back_keep(v):
    return (v, None)

def back_low(kept, grad):
    return (low(grad),)
low.defvjp(low_keep, low_pass)
low_back.defvjp(back_keep, back_low)

def layer_norm(values, gain, shift):
    centred = values - lax.optimization_barrier(jnp.mean(values, axis=-1, keepdims=True))
    spread = lax.optimization_barrier(jnp.mean(centred * centred, axis=-1, keepdims=True))
    return centred * lax.rsqrt(spread + EPSILON) * gain + shift

def product(left_side, right_side):
    return jnp.dot(left_side, right_side, precision=HIGHEST_MODE)

def forward(params, embed_rows, row_mask, key_mask):
    rounded = [low(element) for element in params]
    gain_one, bias_one, query_mat, query_shift, key_mat, value_mat, value_shift, attend_mat, attend_shift, gain_two, bias_two, first_mat, first_shift, second_mat, second_shift = rounded
    slot_count = embed_rows.shape[0]
    width = embed_rows.shape[1]
    normed_one = low(layer_norm(embed_rows, gain_one, bias_one))
    queries = low_back(low(product(normed_one, query_mat) + query_shift))
    key_rows = low_back(low(product(normed_one, key_mat)))
    value_rows = low_back(low(product(normed_one, value_mat) + value_shift))
    query_heads = queries.reshape(slot_count, HEADS, HEAD_DIM)
    key_heads = key_rows.reshape(slot_count, HEADS, HEAD_DIM)
    value_heads = value_rows.reshape(slot_count, HEADS, HEAD_DIM)
    scores = jnp.einsum('qhd,khd->hqk', query_heads, key_heads, precision=HIGHEST_MODE)
    scores = low_back(scores * HEAD_DIM ** (-0.5))
    scores = jnp.where(key_mask[None, None, :], scores, NEGATIVE)
    probs = jax.nn.softmax(scores, axis=-1)
    context = jnp.einsum('hqk,khd->qhd', low(probs), value_heads, precision=HIGHEST_MODE).reshape(slot_count, width)
    context = low_back(low(context))
    attended = low_back(product(context, attend_mat) + attend_shift)
    residual = embed_rows + attended
    normed_two = low(layer_norm(residual, gain_two, bias_two))
    inner = low_back(product(normed_two, first_mat) + first_shift)
    activated = low(jax.nn.gelu(inner, approximate=True))
    mixed = low_back(jnp.dot(activated, second_mat.T, precision=HIGHEST_MODE) + second_shift)
    return (residual + mixed) * row_mask[:, None]

def reference(embeds, image_counts, norm1_gain, norm1_bias, query_weight, query_bias, key_weight, value_weight, value_bias, out_weight, out_bias, norm2_gain, norm2_bias, fc1_weight, fc1_bias, fc2_weight, fc2_bias, out_grad):
    params = (norm1_gain, norm1_bias, query_weight, query_bias, key_weight, value_weight, value_bias, out_weight, out_bias, norm2_gain, norm2_bias, fc1_weight, fc1_bias, fc2_weight, fc2_bias)
    slot_live = jnp.arange(SLOTS, dtype=jnp.int32) < VALID
    image_live = (jnp.arange(IMG_DEV, dtype=jnp.int32)[None, :] < image_counts[:, None]).reshape(IMAGES)

    def step(totals, element):
        embed_rows, grad_rows, live_image = element
        row_mask = jnp.where(slot_live & live_image, 1.0, 0.0).astype(jnp.float32)

        def apply_layer(weights_all, rows_in):
            return forward(weights_all, rows_in, row_mask, slot_live)
        result, pullback = jax.vjp(apply_layer, params, embed_rows)
        param_grads, row_grads = pullback(grad_rows)
        totals = jax.tree.map(lambda first_term, second_term: first_term + second_term, totals, param_grads)
        return (totals, (result.astype(jnp.bfloat16), row_grads.astype(jnp.bfloat16)))
    zero_grads = jax.tree.map(jnp.zeros_like, params)
    totals, outputs_all = lax.scan(step, zero_grads, (embeds.astype(jnp.float32), out_grad.astype(jnp.float32), image_live))
    output, embeds_grad = outputs_all
    return (output, embeds_grad, totals[0], totals[1], totals[2], totals[3], totals[4], totals[5], totals[6], totals[7], totals[8], totals[9], totals[10], totals[11], totals[12], totals[13], totals[14])
```

```python
import jax
import jax.numpy as jnp
from jax import lax
from jax.sharding import PartitionSpec as P

HEAD_DIM = 72
SLOTS = 736
VALID = 729


EPSILON = 1e-06
NEGATIVE = -1000000000.0


def layer_norm(values, gain, shift):
    centred = values - jnp.mean(values, axis=-1, keepdims=True)
    spread = jnp.mean(centred * centred, axis=-1, keepdims=True)
    return centred * lax.rsqrt(spread + EPSILON) * gain + shift


def gelu_tanh(values):
    return jax.nn.gelu(values, approximate=True)


def times_weight(left_side, right_side):
    return jnp.dot(left_side, right_side, preferred_element_type=jnp.float32)


def times_transposed(left_side, right_side):
    return lax.dot_general(
        left_side, right_side, (((1,), (1,)), ((), ())), preferred_element_type=jnp.float32
    )


def outer_sum(left_side, right_side):
    return lax.dot_general(
        left_side, right_side, (((0,), (0,)), ((), ())), preferred_element_type=jnp.float32
    )


def split_heads(stacked):
    slot_count = stacked.shape[1]
    local_heads = stacked.shape[2] // HEAD_DIM
    return (
        stacked[0].reshape(slot_count, local_heads, HEAD_DIM),
        stacked[1].reshape(slot_count, local_heads, HEAD_DIM),
        stacked[2].reshape(slot_count, local_heads, HEAD_DIM),
    )


def head_scores(query_heads, key_heads, slot_live):
    scores = jnp.einsum(
        "qhd,khd->hqk", query_heads, key_heads, preferred_element_type=jnp.float32
    ) * HEAD_DIM ** (-0.5)
    return jnp.where(slot_live[None, None, :], scores, NEGATIVE)


def attend_image(stacked, slot_live):
    query_heads, key_heads, value_heads = split_heads(stacked)
    scores = head_scores(query_heads, key_heads, slot_live)
    highest = jnp.max(scores, axis=-1, keepdims=True)
    raised = jnp.exp(scores - highest)
    total = jnp.sum(raised, axis=-1, keepdims=True)
    probs = (raised / total).astype(jnp.bfloat16)
    context = jnp.einsum("hqk,khd->qhd", probs, value_heads, preferred_element_type=jnp.float32)
    context = context.reshape(stacked.shape[1], stacked.shape[2]).astype(jnp.bfloat16)
    return (context, (highest + jnp.log(total))[..., 0])


def attend_back(stacked, log_total, grad_context, slot_live):
    query_heads, key_heads, value_heads = split_heads(stacked)
    grad_heads = grad_context.reshape(query_heads.shape)
    scores = head_scores(query_heads, key_heads, slot_live)
    probs = jnp.exp(scores - log_total[..., None])
    grad_probs = jnp.einsum(
        "qhd,khd->hqk", grad_heads, value_heads, preferred_element_type=jnp.float32
    )
    row_inner = jnp.sum(probs * grad_probs, axis=-1, keepdims=True)
    grad_scores = (probs * (grad_probs - row_inner)).astype(jnp.bfloat16)
    scale = HEAD_DIM ** (-0.5)
    grad_query = (
        jnp.einsum("hqk,khd->qhd", grad_scores, key_heads, preferred_element_type=jnp.float32)
        * scale
    )
    grad_key = (
        jnp.einsum("hqk,qhd->khd", grad_scores, query_heads, preferred_element_type=jnp.float32)
        * scale
    )
    grad_value = jnp.einsum(
        "hqk,qhd->khd", probs.astype(jnp.bfloat16), grad_heads, preferred_element_type=jnp.float32
    )
    shape_out = (stacked.shape[1], stacked.shape[2])
    return jnp.stack(
        [
            grad_query.reshape(shape_out).astype(jnp.bfloat16),
            grad_key.reshape(shape_out).astype(jnp.bfloat16),
            grad_value.reshape(shape_out).astype(jnp.bfloat16),
        ],
        axis=0,
    )


def per_device(
    embeds,
    image_counts,
    norm1_gain,
    norm1_bias,
    query_weight,
    query_bias,
    key_weight,
    value_weight,
    value_bias,
    out_weight,
    out_bias,
    norm2_gain,
    norm2_bias,
    fc1_weight,
    fc1_bias,
    fc2_weight,
    fc2_bias,
    out_grad,
):
    images, rows_dev, width = embeds.shape
    token_count = images * rows_dev
    columns = query_weight.shape[1]
    hidden = fc1_weight.shape[1]
    position = lax.axis_index("seq") * rows_dev + jnp.arange(rows_dev, dtype=jnp.int32)
    slot_live = jnp.arange(SLOTS, dtype=jnp.int32) < VALID
    image_live = jnp.arange(images, dtype=jnp.int32) < image_counts[0]
    row_mask = (
        jnp.where(image_live[:, None] & (position < VALID)[None, :], 1.0, 0.0)
        .astype(jnp.float32)
        .reshape(token_count)
    )
    low = jnp.bfloat16
    attention_low = jnp.concatenate([query_weight, key_weight, value_weight], axis=1).astype(low)
    attention_full = lax.all_gather(attention_low, "dp", axis=0, tiled=True)
    rest_low = jnp.concatenate([out_weight, fc1_weight, fc2_weight], axis=1).astype(low)
    rest_full = lax.all_gather(rest_low, "dp", axis=0, tiled=True)
    out_part = rest_full[:, :columns]
    first_part = rest_full[:, columns : columns + hidden]
    second_part = rest_full[:, columns + hidden :]
    packed = jnp.stack(
        [norm1_gain, norm1_bias, out_bias, norm2_gain, norm2_bias, fc2_bias], axis=0
    ).astype(low)
    vectors = lax.all_gather(packed, "seq", axis=1, tiled=True).astype(jnp.float32)
    gain_one, bias_one, attend_shift, gain_two, bias_two, second_shift = [vectors[i] for i in range(6)]
    query_shift = query_bias.astype(low).astype(jnp.float32)
    value_shift = value_bias.astype(low).astype(jnp.float32)
    first_shift = fc1_bias.astype(low).astype(jnp.float32)

    embed_rows = embeds.reshape(token_count, width).astype(jnp.float32)
    normed_one = layer_norm(embed_rows, gain_one, bias_one).astype(low)
    one_all = lax.all_gather(
        normed_one.reshape(images, rows_dev, width), "seq", axis=1, tiled=True
    ).reshape(images * SLOTS, width)
    grad_mixed = out_grad.reshape(token_count, width).astype(jnp.float32) * row_mask[:, None]
    grad_mixed_low = grad_mixed.astype(low)
    mixed_all = lax.all_gather(
        grad_mixed_low.reshape(images, rows_dev, width), "seq", axis=1, tiled=True
    ).reshape(images * SLOTS, width)

    shift_all = jnp.concatenate([query_shift, jnp.zeros_like(query_shift), value_shift])
    heads_all = (times_weight(one_all, attention_full) + shift_all).astype(low)
    by_heads = heads_all.reshape(images, SLOTS, 3, columns).transpose(0, 2, 1, 3)
    context_heads, log_total = lax.map(lambda element: attend_image(element, slot_live), by_heads)
    context = lax.all_to_all(context_heads, "seq", split_axis=1, concat_axis=2, tiled=True).reshape(
        token_count, width
    )
    out_full = lax.all_gather(out_part, "seq", axis=1, tiled=True)
    residual = embed_rows + times_weight(context, out_full) + attend_shift
    normed_two = layer_norm(residual, gain_two, bias_two).astype(low)
    two_all = lax.all_gather(
        normed_two.reshape(images, rows_dev, width), "seq", axis=1, tiled=True
    ).reshape(images * SLOTS, width)
    inner = times_weight(two_all, first_part) + first_shift
    activated = gelu_tanh(inner).astype(low)
    grad_active = times_weight(mixed_all, second_part)
    grad_inner = jax.vjp(gelu_tanh, inner)[1](grad_active)[0].astype(low)

    def scatter_rows(partial):
        parts = partial.astype(low).reshape(images, SLOTS, width)
        arrived = lax.all_to_all(
            parts.reshape(images, -1, rows_dev, width), "seq", split_axis=1, concat_axis=1, tiled=True
        )
        return jnp.sum(arrived.astype(jnp.float32), axis=1).reshape(token_count, width)

    grad_normed_two = scatter_rows(times_transposed(grad_inner, first_part))
    mixed = scatter_rows(times_transposed(activated, second_part)) + second_shift
    output = (
        ((residual + mixed) * row_mask[:, None]).astype(low).reshape(images, rows_dev, width)
    )
    second_shift_grad = jnp.sum(grad_mixed, axis=0)
    norm_two_pull = jax.vjp(layer_norm, residual, gain_two, bias_two)[1]
    grad_norm_input, gain_two_grad, bias_two_grad = norm_two_pull(grad_normed_two)
    grad_residual = grad_mixed + grad_norm_input
    grad_attended = grad_residual.astype(low)
    attended_all = lax.all_gather(
        grad_attended.reshape(images, rows_dev, width), "seq", axis=1, tiled=True
    ).reshape(images * SLOTS, width)
    out_rows = lax.dynamic_slice_in_dim(
        out_full, lax.axis_index("seq") * columns, columns, axis=0
    )
    grad_context = times_transposed(attended_all, out_rows).astype(low)
    fc_grads = jnp.concatenate(
        [outer_sum(two_all, grad_inner).astype(low), outer_sum(mixed_all, activated).astype(low)], axis=1
    )
    fc_owned = lax.psum_scatter(fc_grads, "dp", scatter_dimension=0, tiled=True).astype(jnp.float32)
    out_grad_rows = outer_sum(context_heads.reshape(images * SLOTS, columns), attended_all).astype(low)
    out_grad_cols = lax.all_to_all(out_grad_rows, "seq", split_axis=1, concat_axis=0, tiled=True)
    grad_stacked = lax.map(
        lambda element: attend_back(element[0], element[1], element[2], slot_live),
        (by_heads, log_total, grad_context.reshape(images, SLOTS, columns)),
    )
    grad_heads_all = grad_stacked.transpose(0, 2, 1, 3).reshape(images * SLOTS, 3 * columns)
    attention_grads = jnp.concatenate(
        [outer_sum(one_all, grad_heads_all).astype(low), out_grad_cols], axis=1
    )
    attention_owned = lax.psum_scatter(
        attention_grads, "dp", scatter_dimension=0, tiled=True
    ).astype(jnp.float32)
    grad_normed_one = scatter_rows(times_transposed(grad_heads_all, attention_full))
    norm_one_pull = jax.vjp(layer_norm, embed_rows, gain_one, bias_one)[1]
    grad_embed_norm, gain_one_grad, bias_one_grad = norm_one_pull(grad_normed_one)
    embeds_grad = (grad_residual + grad_embed_norm).astype(low).reshape(images, rows_dev, width)
    whole = jnp.stack(
        [
            gain_one_grad,
            bias_one_grad,
            jnp.sum(grad_attended.astype(jnp.float32), axis=0),
            gain_two_grad,
            bias_two_grad,
            second_shift_grad,
        ],
        axis=0,
    )
    owned = lax.psum_scatter(whole, "seq", scatter_dimension=1, tiled=True)
    head_sums = jnp.sum(grad_heads_all.astype(jnp.float32), axis=0)
    query_shift_grad = head_sums[:columns]
    value_shift_grad = head_sums[2 * columns :]
    first_shift_grad = jnp.sum(grad_inner.astype(jnp.float32), axis=0)
    owned, query_shift_grad, value_shift_grad, first_shift_grad = lax.psum(
        (owned, query_shift_grad, value_shift_grad, first_shift_grad), "dp"
    )
    return (
        output,
        embeds_grad,
        owned[0],
        owned[1],
        attention_owned[:, :columns],
        query_shift_grad,
        attention_owned[:, columns : 2 * columns],
        attention_owned[:, 2 * columns : 3 * columns],
        value_shift_grad,
        attention_owned[:, 3 * columns :],
        owned[2],
        owned[3],
        owned[4],
        fc_owned[:, :hidden],
        first_shift_grad,
        fc_owned[:, hidden:],
        owned[5],
    )


def solution(mesh):
    in_specs = (
        P("dp", "seq", None),
        P("dp"),
        P("seq"),
        P("seq"),
        P("dp", "seq"),
        P("seq"),
        P("dp", "seq"),
        P("dp", "seq"),
        P("seq"),
        P("dp", "seq"),
        P("seq"),
        P("seq"),
        P("seq"),
        P("dp", "seq"),
        P("seq"),
        P("dp", "seq"),
        P("seq"),
        P("dp", "seq", None),
    )
    out_specs = (
        P("dp", "seq", None),
        P("dp", "seq", None),
        P("seq"),
        P("seq"),
        P("dp", "seq"),
        P("seq"),
        P("dp", "seq"),
        P("dp", "seq"),
        P("seq"),
        P("dp", "seq"),
        P("seq"),
        P("seq"),
        P("seq"),
        P("dp", "seq"),
        P("seq"),
        P("dp", "seq"),
        P("seq"),
    )
    return jax.shard_map(
        per_device, mesh=mesh, in_specs=in_specs, out_specs=out_specs, check_vma=False
    )
```
